32 devices in a mesh: pair: 2 (over x), day: 4 (over z), lag: 4 (over y, core).
Axes of the slice: x: 2, y: 2, z: 4, core: 2. Of those that a mesh axis runs over, the one named last changes fastest.
Arguments:
- corr: bfloat16 [2048, 16, 2048], P('pair', 'day', 'lag'), may hold values from -150 to 150
Outputs:
- pws_stack: float32 [2048, 2048], P('pair', 'lag')
- robust_stack: float32 [2048, 2048], P('pair', 'lag')
- day_weights: float32 [2048, 16], P('pair', 'day')
The draws below stay inside these ranges and needn't reach their ends.
All inputs are finite; a program needn't handle non-finite values.
Results may differ from the reference program's by a relative error of at most 0.00049.
Values may be sent and summed in bfloat16 or wider, within the bound.
No kernel may reach another device: no remote copies, remote signals or barrier semaphores. Data moves between devices by JAX's collectives and lax.ppermute only.
A program may use at most 128 MiB of HBM per device.

```python
import math
import jax
import jax.numpy as jnp
from jax import lax

LAGS = 2048
ITERS = 3
PAIRS = 2048
DAYS = 16


def smooth_rows(values, width):
    extended = jnp.concatenate([values, values[..., :width]], axis=-1)
    running = jnp.cumsum(extended, axis=-1)
    leading = jnp.zeros(values.shape[:-1] + (1,), jnp.float32)
    running = jnp.concatenate([leading, running], axis=-1)
    return (running[..., width:width + LAGS] - running[..., :LAGS]) / width


def draw_corr(key, part):
    streams = jax.random.split(key, 11)
    width = max(LAGS // 32, 2)
    white = jax.random.truncated_normal(streams[0], -4.0, 4.0, (PAIRS, 3, LAGS), jnp.float32)
    smooth = smooth_rows(smooth_rows(white, width), width)
    smooth = smooth / jnp.sqrt(jnp.mean(smooth * smooth, axis=2, keepdims=True) + 1e-06)
    position = jnp.arange(LAGS, dtype=jnp.int32)
    centre = jax.random.randint(streams[1], (PAIRS, 1), 0, max(LAGS // 16, 1))
    spread = LAGS / 20.0

    def envelope(middle):
        offset = (position[None, :] - middle) % LAGS
        distance = jnp.minimum(offset, LAGS - offset).astype(jnp.float32)
        return jnp.exp(-(distance / spread) ** 2)
    signs = jnp.where(jax.random.uniform(streams[2], (PAIRS, 2), jnp.float32) < 0.5, -1.0, 1.0)
    causal = signs[:, 0:1] * envelope(centre) * (0.8 + smooth[:, 0, :])
    acausal = signs[:, 1:2] * envelope(centre + LAGS // 2) * (0.8 + smooth[:, 1, :])
    coda = 0.15 * smooth[:, 2, :]
    fraction = jax.random.uniform(streams[3], (PAIRS, 1), jnp.float32, 0.25, 0.75)
    season = jax.random.uniform(streams[4], (PAIRS, DAYS), jnp.float32) < fraction
    weight_causal = jnp.where(season, 1.0, 0.25)
    weight_acausal = jnp.where(season, 0.25, 1.0)
    signal = weight_causal[:, :, None] * causal[:, None, :] + weight_acausal[:, :, None] * acausal[:, None, :] + coda[:, None, :]
    amplitude = jnp.exp(jax.random.uniform(streams[5], (PAIRS, DAYS, 1), jnp.float32, math.log(0.05), math.log(2.0)))
    polarity = jnp.where(jax.random.uniform(streams[6], (PAIRS, DAYS, 1), jnp.float32) < 0.15, -1.0, 1.0)
    ramp = 1.0 + 2.0 * jnp.arange(DAYS, dtype=jnp.float32) / max(DAYS - 1, 1)
    day_scale = jnp.exp(jax.random.uniform(streams[7], (PAIRS, DAYS, 1), jnp.float32, math.log(0.1), math.log(3.0))) * ramp[None, :, None]
    lag_scale = jnp.exp(jax.random.uniform(streams[8], (PAIRS, 1, LAGS), jnp.float32, math.log(0.5), math.log(5.0)))
    noise = jax.random.truncated_normal(streams[10], -4.0, 4.0, (PAIRS, DAYS, LAGS), jnp.float32)
    return (amplitude * polarity * signal + 0.06 * noise * day_scale * lag_scale).astype(jnp.bfloat16)


def setup_inputs(seed: int = 0) -> dict:
    key_list = jax.random.split(jax.random.key(seed), 2)
    corr = draw_corr(jax.random.fold_in(key_list[1], 71), 0)
    return dict(corr=corr)


epsilon = 1e-06

def kernel_block(rows, cols, lags):
    offset = (cols[None, :] - rows[:, None]) % lags
    odd = offset % 2 == 1
    angle = jnp.pi * offset.astype(jnp.float32) / lags
    value = jnp.where(odd, 2.0 / lags * jnp.cos(angle) / jnp.where(odd, jnp.sin(angle), 1.0), 0.0)
    return value.astype(jnp.bfloat16)

def reference(corr):
    data = corr.astype(jnp.float32)
    norm2 = lax.optimization_barrier(jnp.sum(data * data, axis=2))
    rms = jnp.sqrt(norm2 / LAGS + epsilon)
    xn = data / rms[:, :, None]
    index = jnp.arange(LAGS, dtype=jnp.int32)
    kernel = lax.optimization_barrier(kernel_block(index, index, LAGS)).astype(jnp.float32)
    quad = jnp.dot(data.reshape(-1, LAGS), kernel, precision=lax.Precision.HIGHEST).reshape(data.shape)
    den = jnp.maximum(jnp.sqrt(data * data + quad * quad), 0.1 * rms[:, :, None])
    cosine = data / den
    sine = quad / den
    linear = lax.optimization_barrier(jnp.sum(xn, axis=1))
    csum = lax.optimization_barrier(jnp.sum(cosine, axis=1))
    ssum = lax.optimization_barrier(jnp.sum(sine, axis=1))
    pws = linear / DAYS * ((csum * csum + ssum * ssum) / (DAYS * DAYS))
    stack = pws
    weight = jnp.zeros((PAIRS, DAYS), jnp.float32)
    total = jnp.ones((PAIRS,), jnp.float32)
    for step in range(ITERS):
        msq = lax.optimization_barrier(jnp.sum(stack * stack, axis=1)) / LAGS
        normed = stack / jnp.sqrt(msq + epsilon)[:, None]
        coh = lax.optimization_barrier(jnp.sum(xn * normed[:, None, :], axis=2)) / LAGS
        res = lax.optimization_barrier(jnp.sum((xn - coh[:, :, None] * normed[:, None, :]) ** 2, axis=2)) / LAGS
        rbar = lax.optimization_barrier(jnp.sum(res, axis=1)) / DAYS
        weight = (0.1 + jnp.abs(coh)) / (res + rbar[:, None] + epsilon)
        stack = lax.optimization_barrier(jnp.sum(weight[:, :, None] * xn, axis=1))
        total = lax.optimization_barrier(jnp.sum(weight, axis=1))
    return (pws, stack / total[:, None], weight / total[:, None])
```

```python
import functools

import jax
import jax.numpy as jnp
from jax import lax
from jax.experimental import pallas as pl
from jax.experimental.pallas import tpu as pltpu
from jax.sharding import PartitionSpec as P

ITERS = 3
LANES = 128
epsilon = 1e-06


def kernel_rows(rows, lags):
    row = jnp.arange(rows, dtype=jnp.int32)
    col = jnp.arange(lags, dtype=jnp.int32)
    offset = (col[None, :] - row[:, None]) % lags
    odd = offset % 2 == 1
    angle = jnp.pi * offset.astype(jnp.float32) / lags
    value = jnp.where(odd, 2.0 / lags * jnp.cos(angle) / jnp.where(odd, jnp.sin(angle), 1.0), 0.0)
    return value.astype(jnp.bfloat16)


def stack_kernel(sizes, top_ref, *refs):
    n_src, lag_groups, days_here, group, lags = sizes
    ins = refs[:n_src]
    pws_ref, robust_ref, share_ref = refs[n_src:n_src + 3]
    matrix, rows32, data, data16, quad, normed, stack = refs[n_src + 3:]
    days = n_src // lag_groups * days_here
    width = lags // lag_groups
    tiles = width // LANES
    top_rows = top_ref.shape[0]
    pitch = tiles * days_here

    @pl.when(pl.program_id(0) == 0)
    def _():
        for a in range(lags // top_rows):
            cut = a * top_rows
            if cut:
                matrix[cut:cut + top_rows, :cut] = top_ref[:, lags - cut:]
            matrix[cut:cut + top_rows, cut:] = top_ref[:, :lags - cut]

    for s in range(n_src):
        block, part = divmod(s, lag_groups)
        rows32[...] = ins[s][...].astype(jnp.float32)
        for d in range(days_here):
            day = block * days_here + d
            for t in range(tiles):
                lane = part * width + t * LANES
                x = rows32[pl.ds(t * days_here + d, group, stride=pitch), :]
                data[day, :, lane:lane + LANES] = x
                data16[day * group:(day + 1) * group, lane:lane + LANES] = x.astype(jnp.bfloat16)

    quad[...] = jnp.dot(data16[...], matrix[...], preferred_element_type=jnp.float32)

    scale = []
    for day in range(days):
        x = data[day]
        norm2 = jnp.sum(x * x, axis=1, keepdims=True)
        scale.append(1.0 / jnp.sqrt(norm2 / lags + epsilon))

    chunk = min(512, lags)
    for c in range(0, lags, chunk):
        linear = csum = ssum = None
        for day in range(days):
            x = data[day, :, c:c + chunk]
            q = quad[day * group:(day + 1) * group, c:c + chunk]
            inv = jnp.minimum(lax.rsqrt(x * x + q * q), 10.0 * scale[day])
            xn = x * scale[day]
            data[day, :, c:c + chunk] = xn
            if day == 0:
                linear, csum, ssum = xn, x * inv, q * inv
            else:
                linear, csum, ssum = linear + xn, csum + x * inv, ssum + q * inv
        pws = linear / days * ((csum * csum + ssum * ssum) / (days * days))
        stack[:, c:c + chunk] = pws
    pws_ref[...] = stack[...]

    total = None
    weights = None
    for step in range(ITERS):
        s = stack[...]
        msq = jnp.sum(s * s, axis=1, keepdims=True) / lags
        normed[...] = s * (1.0 / jnp.sqrt(msq + epsilon))
        cohs, ress = [], []
        for day in range(days):
            coh = jnp.sum(data[day] * normed[...], axis=1, keepdims=True) / lags
            cohs.append(coh)
        for day in range(days):
            gap = data[day] - cohs[day] * normed[...]
            ress.append(jnp.sum(gap * gap, axis=1, keepdims=True) / lags)
        rbar = sum(ress[1:], ress[0]) / days
        weights = [(0.1 + jnp.abs(c)) / (r + rbar + epsilon) for c, r in zip(cohs, ress)]
        total = sum(weights[1:], weights[0])
        last = step == ITERS - 1
        if last:
            weights = [w / total for w in weights]
        for c in range(0, lags, chunk):
            acc = weights[0] * data[0, :, c:c + chunk]
            for day in range(1, days):
                acc = acc + weights[day] * data[day, :, c:c + chunk]
            if last:
                robust_ref[:, c:c + chunk] = acc
            else:
                stack[:, c:c + chunk] = acc
    share_ref[...] = jnp.concatenate(weights, axis=1)


def stack_pairs(pieces, top, lag_groups, days_here, pairs, group):
    n_src = len(pieces)
    lags = top.shape[1]
    days = n_src // lag_groups * days_here
    pitch = lags // lag_groups // LANES * days_here
    sizes = (n_src, lag_groups, days_here, group, lags)
    cost = pl.CostEstimate(
        flops=2 * pairs * days * lags * lags, bytes_accessed=pairs * days * lags * 2, transcendentals=pairs * days * lags
    )
    return pl.pallas_call(
        functools.partial(stack_kernel, sizes),
        grid=(pairs // group,),
        in_specs=[pl.BlockSpec(top.shape, lambda i: (0, 0))]
        + [pl.BlockSpec((group * pitch, LANES), lambda i: (i, 0))] * n_src,
        out_specs=[
            pl.BlockSpec((group, lags), lambda i: (i, 0)),
            pl.BlockSpec((group, lags), lambda i: (i, 0)),
            pl.BlockSpec((group, days), lambda i: (i, 0)),
        ],
        out_shape=[
            jax.ShapeDtypeStruct((pairs, lags), jnp.float32),
            jax.ShapeDtypeStruct((pairs, lags), jnp.float32),
            jax.ShapeDtypeStruct((pairs, days), jnp.float32),
        ],
        scratch_shapes=[
            pltpu.VMEM((lags, lags), jnp.bfloat16),
            pltpu.VMEM((group * pitch, LANES), jnp.float32),
            pltpu.VMEM((days, group, lags), jnp.float32),
            pltpu.VMEM((days * group, lags), jnp.bfloat16),
            pltpu.VMEM((days * group, lags), jnp.float32),
            pltpu.VMEM((group, lags), jnp.float32),
            pltpu.VMEM((group, lags), jnp.float32),
        ],
        cost_estimate=cost,
        name="stack_pairs",
    )(top, *pieces)


def per_device(corr):
    pairs, days_here, width = corr.shape
    lag_groups = lax.axis_size("lag")
    day_groups = lax.axis_size("day")
    n = lag_groups * day_groups
    lags = width * lag_groups
    mine = pairs // n
    tiles = width // LANES
    top = kernel_rows(min(256, lags), lags)
    moved = lax.all_to_all(corr, ("day", "lag"), 0, 0, tiled=True)
    moved = moved.reshape(n, mine, days_here, tiles, LANES).transpose(0, 1, 3, 2, 4)
    moved = moved.reshape(n, mine * tiles * days_here, LANES)
    pieces = [moved[s] for s in range(n)]
    pws, robust, shares = stack_pairs(pieces, top, lag_groups, days_here, mine, 16)
    both = jnp.stack([pws, robust])
    peak = jnp.maximum(jnp.max(jnp.abs(both), axis=2), 1e-30)
    both = (both * (1024.0 / peak)[:, :, None]).astype(jnp.float16)
    both = both.reshape(2, mine, lag_groups, width).transpose(2, 0, 1, 3)
    both = jnp.broadcast_to(both[None], (day_groups,) + both.shape).reshape((n,) + both.shape[1:])
    both = lax.all_to_all(both, ("day", "lag"), 0, 0, tiled=True)
    side = jnp.concatenate([shares, peak.T / 1024.0], axis=1)
    side = lax.all_gather(side, ("day", "lag"), axis=0, tiled=True)
    days = days_here * day_groups
    both = both.transpose(1, 0, 2, 3).reshape(2, pairs, width).astype(jnp.float32)
    first = lax.axis_index("day") * days_here
    return (
        both[0] * side[:, days:days + 1],
        both[1] * side[:, days + 1:],
        lax.dynamic_slice_in_dim(side, first, days_here, 1),
    )


def solution(mesh):
    return jax.shard_map(
        per_device,
        mesh=mesh,
        in_specs=(P("pair", "day", "lag"),),
        out_specs=(P("pair", "lag"), P("pair", "lag"), P("pair", "day")),
        check_vma=False,
    )
```

```python
import functools

import jax
import jax.numpy as jnp
from jax import lax
from jax.experimental import pallas as pl
from jax.experimental.pallas import tpu as pltpu
from jax.sharding import PartitionSpec as P


ITERS = 3
LANES = 128
SUBLANES = 8
PLAN = ((32, "all", "staged"), (16, "all", "staged"), (16, "all", "all"),)
epsilon = 1e-06


def kernel_rows(rows, lags):
    row = jnp.arange(rows, dtype=jnp.int32)
    col = jnp.arange(lags, dtype=jnp.int32)
    offset = (col[None, :] - row[:, None]) % lags
    odd = offset % 2 == 1
    angle = jnp.pi * offset.astype(jnp.float32) / lags
    value = jnp.where(odd, 2.0 / lags * jnp.cos(angle) / jnp.where(odd, jnp.sin(angle), 1.0), 0.0)
    return value.astype(jnp.bfloat16)


def stack_kernel(sizes, me_ref, top_ref, *refs):
    lag_groups, days_here, group, lags, n_src = sizes
    ins = refs[:-8]
    message_ref, matrix, rows32, data, data16, quad, normed, stack = refs[-8:]
    days = n_src // lag_groups * days_here
    width = lags // lag_groups
    tiles = width // LANES
    top_rows = top_ref.shape[0]
    pitch = tiles * days_here
    chunk = min(512, width)

    @pl.when(pl.program_id(0) == 0)
    def _():
        for a in range(lags // top_rows):
            cut = a * top_rows
            if cut:
                matrix[cut:cut + top_rows, :cut] = top_ref[:, lags - cut:]
            matrix[cut:cut + top_rows, cut:] = top_ref[:, :lags - cut]

    for s in range(n_src):
        if len(ins) == 1:
            here = pl.multiple_of(pl.program_id(0) * group * pitch, group * pitch)
            rows32[...] = ins[0][s, pl.ds(here, group * pitch), :].astype(jnp.float32)
            block, part = divmod(s, lag_groups)
        else:
            rows32[...] = ins[s][...].astype(jnp.float32)
            source = me_ref[0] ^ s
            block, part = source // lag_groups, source % lag_groups
        for d in range(days_here):
            day = block * days_here + d
            row = pl.multiple_of(day * group, group)
            for t in range(tiles):
                lane = pl.ds(pl.multiple_of(part * width + t * LANES, LANES), LANES)
                x = rows32[pl.ds(t * days_here + d, group, stride=pitch), :]
                data[day, :, lane] = x
                data16[pl.ds(row, group), lane] = x.astype(jnp.bfloat16)

    quad[...] = jnp.dot(data16[...], matrix[...], preferred_element_type=jnp.float32)

    scale = []
    for day in range(days):
        x = data[day]
        norm2 = jnp.sum(x * x, axis=1, keepdims=True)
        scale.append(1.0 / jnp.sqrt(norm2 / lags + epsilon))

    for c in range(0, lags, chunk):
        linear = csum = ssum = None
        for day in range(days):
            x = data[day, :, c:c + chunk]
            q = quad[day * group:(day + 1) * group, c:c + chunk]
            inv = jnp.minimum(lax.rsqrt(x * x + q * q), 10.0 * scale[day])
            xn = x * scale[day]
            data[day, :, c:c + chunk] = xn
            if day == 0:
                linear, csum, ssum = xn, x * inv, q * inv
            else:
                linear, csum, ssum = linear + xn, csum + x * inv, ssum + q * inv
        stack[:, c:c + chunk] = linear / days * ((csum * csum + ssum * ssum) / (days * days))

    bands = group // SUBLANES
    all_bands = bands * pl.num_programs(0)

    def emit(kind, value):
        peak = jnp.maximum(jnp.max(jnp.abs(value), axis=1, keepdims=True), 1e-30)
        power = jnp.floor(jnp.log2(peak))
        value = value * jnp.exp2(9.0 - power)
        for part in range(lag_groups):
            for r in range(bands):
                for t in range(tiles):
                    place = (kind * all_bands + pl.program_id(0) * bands + r) * tiles + t
                    lane = part * width + t * LANES
                    message_ref[part, place] = value[r * SUBLANES:(r + 1) * SUBLANES, lane:lane + LANES]
        return power

    powers = [emit(0, stack[...])]
    for step in range(ITERS):
        s = stack[...]
        msq = jnp.sum(s * s, axis=1, keepdims=True) / lags
        normed[...] = s * (1.0 / jnp.sqrt(msq + epsilon))
        cohs, ress = [], []
        for day in range(days):
            cohs.append(jnp.sum(data[day] * normed[...], axis=1, keepdims=True) / lags)
        for day in range(days):
            gap = data[day] - cohs[day] * normed[...]
            ress.append(jnp.sum(gap * gap, axis=1, keepdims=True) / lags)
        rbar = sum(ress[1:], ress[0]) / days
        weights = [(0.1 + jnp.abs(c)) / (r + rbar + epsilon) for c, r in zip(cohs, ress)]
        if step == ITERS - 1:
            total = sum(weights[1:], weights[0])
            weights = [w / total for w in weights]
        for c in range(0, lags, chunk):
            acc = weights[0] * data[0, :, c:c + chunk]
            for day in range(1, days):
                acc = acc + weights[day] * data[day, :, c:c + chunk]
            stack[:, c:c + chunk] = acc
    powers.append(emit(1, stack[...]))
    side = jnp.concatenate([w * 1024.0 for w in weights] + powers, axis=1)
    per = LANES // (days + 2)
    for r in range(bands):
        band = pl.program_id(0) * bands + r
        for k in range(per):
            @pl.when(band % per == k)
            def _():
                for part in range(lag_groups):
                    message_ref[part, 2 * tiles * all_bands + band // per, :, k * (days + 2):(k + 1) * (days + 2)] = (
                        side[r * SUBLANES:(r + 1) * SUBLANES])


def stack_pairs(me, pieces, top, lag_groups, days_here, pairs, group, n_src):
    lags = top.shape[1]
    days = n_src // lag_groups * days_here
    width = lags // lag_groups
    pitch = width // LANES * days_here
    bands = pairs // SUBLANES
    tiles = 2 * bands * (width // LANES) + pl.cdiv(bands, LANES // (days + 2))
    cost = pl.CostEstimate(
        flops=2 * pairs * days * lags * lags, bytes_accessed=pairs * days * lags * 2, transcendentals=pairs * days * lags
    )
    if len(pieces) == 1:
        piece_specs = [pl.BlockSpec(memory_space=pltpu.VMEM)]
    else:
        piece_specs = [pl.BlockSpec((group * pitch, LANES), lambda i: (i, 0))] * n_src
    return pl.pallas_call(
        functools.partial(stack_kernel, (lag_groups, days_here, group, lags, n_src)),
        grid=(pairs // group,),
        in_specs=[pl.BlockSpec(memory_space=pltpu.SMEM), pl.BlockSpec(top.shape, lambda i: (0, 0))] + piece_specs,
        out_specs=pl.BlockSpec(memory_space=pltpu.VMEM),
        out_shape=jax.ShapeDtypeStruct((lag_groups, tiles, SUBLANES, LANES), jnp.float32),
        scratch_shapes=[
            pltpu.VMEM((lags, lags), jnp.bfloat16),
            pltpu.VMEM((group * pitch, LANES), jnp.float32),
            pltpu.VMEM((days, group, lags), jnp.float32),
            pltpu.VMEM((days * group, lags), jnp.bfloat16),
            pltpu.VMEM((days * group, lags), jnp.float32),
            pltpu.VMEM((group, lags), jnp.float32),
            pltpu.VMEM((group, lags), jnp.float32),
        ],
        cost_estimate=cost,
        name="stack_pairs",
    )(me, top, *pieces)


def unpack(message, pairs, width, days, days_here):
    n = message.shape[0]
    bands, tiles, per = pairs // SUBLANES, width // LANES, LANES // (days + 2)
    side = message[:, 2 * bands * tiles:].astype(jnp.float32)
    blocks = [side[:, r // per, :, r % per * (days + 2):(r % per + 1) * (days + 2)] for r in range(bands)]
    blocks = jnp.stack(blocks, axis=1)
    shares = lax.dynamic_slice_in_dim(blocks, lax.axis_index("day") * days_here, days_here, 3) / 1024.0
    outs = []
    for kind in range(2):
        scale = jnp.exp2(blocks[:, :, :, days + kind] - 9.0)
        scale = jnp.broadcast_to(scale[:, :, None, :, None], (n, bands, 1, SUBLANES, LANES))
        scale = lax.optimization_barrier(scale)
        value = message[:, kind * bands * tiles:(kind + 1) * bands * tiles].astype(jnp.float32)
        value = value.reshape(n, bands, tiles, SUBLANES, LANES) * scale
        outs.append(jnp.swapaxes(value, 2, 3).reshape(n * pairs, width))
    return outs[0], outs[1], shares.reshape(n * pairs, days_here)


AXES = ("day", "lag")


def swap(x, n, by):
    return lax.ppermute(x, AXES, [(i, i ^ by) for i in range(n)])


def spread_direct(message, day_groups, n):
    message = jnp.broadcast_to(message[None], (day_groups,) + message.shape).reshape((n,) + message.shape[1:])
    return lax.all_to_all(message, AXES, 0, 0, tiled=True)


def unswap(pieces, index):
    step = 1
    while step < len(pieces):
        odd = (index // step) % 2 == 1
        pieces = [jnp.where(odd, pieces[k ^ step], pieces[k]) for k in range(len(pieces))]
        step *= 2
    return pieces


def spread_lags(message, me, lag_groups, n):
    lag = me % lag_groups
    pieces = unswap([message[m] for m in range(lag_groups)], lag)
    got = [pieces[0]] + [swap(pieces[m], n, m) for m in range(1, lag_groups)]
    return jnp.stack(unswap(got, lag))


def spread_days(got, me, lag_groups, n):
    near, far = me // lag_groups % 2, me // (2 * lag_groups)
    got = jnp.stack(unswap([got, swap(got, n, 2 * lag_groups)], far))
    got = jnp.stack(unswap([got, swap(got, n, lag_groups)], near), axis=1)
    return got.reshape((n,) + got.shape[3:])


def per_device(corr):
    pairs, days_here, width = corr.shape
    lag_groups = lax.axis_size("lag")
    day_groups = lax.axis_size("day")
    n = lag_groups * day_groups
    me = lax.axis_index(AXES)
    lags = width * lag_groups
    days = days_here * day_groups
    tiles = width // LANES
    top = kernel_rows(min(256, lags), lags)
    mine = pairs // n
    staged = day_groups == 4 and lag_groups == 4 and mine == sum(p for p, _, _ in PLAN)
    plan = PLAN if staged else ((mine, "all", "all"),)

    def flat(piece, lead):
        piece = piece.reshape(lead + (piece.shape[-3], days_here, tiles, LANES))
        piece = jnp.swapaxes(piece, -2, -3)
        return piece.reshape(lead + (-1, LANES))

    outs = [jnp.zeros((pairs, width), jnp.float32), jnp.zeros((pairs, width), jnp.float32)]
    starts = [sum(p for p, _, _ in plan[:k]) for k in range(len(plan))]
    moved, sent = [], []

    def work(k):
        message = stack_pairs(me.reshape(1), moved[k], top, lag_groups, days_here, plan[k][0], 16 if plan[k][0] % 16 == 0 else 8, n)
        message = message.astype(jnp.float16)
        if plan[k][2] == "staged":
            message = spread_lags(message, me, lag_groups, n)
        sent.append(message)

    for k, (p, _, _) in enumerate(plan):
        if k >= 2:
            work(k - 2)
        if k == 1:
            corr, top, *outs = lax.optimization_barrier((corr, top, *outs))
        rows = corr[starts[k] * n:(starts[k] + p) * n]
        if k >= 1:
            rows, moved[k - 1] = lax.optimization_barrier((rows, moved[k - 1]))
        if k >= 2:
            rows, sent[k - 2] = lax.optimization_barrier((rows, sent[k - 2]))
        got = lax.all_to_all(rows, AXES, 0, 0, tiled=True)
        moved.append([flat(got.reshape(n, p, days_here, width), (n,))])
    for k in range(len(sent), len(plan)):
        work(k)
    outs = list(outs) + [jnp.zeros((pairs, days_here), jnp.float32)]
    for k, (p, _, how) in enumerate(plan):
        spread = spread_direct(sent[k], day_groups, n) if how == "all" else spread_days(sent[k], me, lag_groups, n)
        parts = unpack(spread, p, width, days, days_here)
        outs = [lax.dynamic_update_slice(o, v, (starts[k] * n, 0)) for o, v in zip(outs, parts)]
    return tuple(outs)


def solution(mesh):
    return jax.shard_map(
        per_device,
        mesh=mesh,
        in_specs=(P("pair", "day", "lag"),),
        out_specs=(P("pair", "lag"), P("pair", "lag"), P("pair", "day")),
        check_vma=False,
    )
```

```python
import functools

import jax
import jax.numpy as jnp
from jax import lax
from jax.experimental import pallas as pl
from jax.experimental.pallas import tpu as pltpu
from jax.sharding import PartitionSpec as P


ITERS = 3
LANES = 128
SUBLANES = 8
PLAN = ((32, "all", "staged"), (16, "all", "staged"), (16, "all", "all"),)
epsilon = 1e-06


def kernel_rows(rows, lags):
    row = jnp.arange(rows, dtype=jnp.int32)
    col = jnp.arange(lags, dtype=jnp.int32)
    offset = (col[None, :] - row[:, None]) % lags
    odd = offset % 2 == 1
    angle = jnp.pi * offset.astype(jnp.float32) / lags
    value = jnp.where(odd, 2.0 / lags * jnp.cos(angle) / jnp.where(odd, jnp.sin(angle), 1.0), 0.0)
    return value.astype(jnp.bfloat16)


def stack_kernel(sizes, top_ref, moved_ref, message_ref, matrix, rows32, data, data16, quad, normed, stack):
    lag_groups, days_here, group, lags, n_src = sizes
    days = n_src // lag_groups * days_here
    width = lags // lag_groups
    tiles = width // LANES
    top_rows = top_ref.shape[0]
    pitch = tiles * days_here
    chunk = min(512, width)

    @pl.when(pl.program_id(0) == 0)
    def _():
        for a in range(lags // top_rows):
            cut = a * top_rows
            if cut:
                matrix[cut:cut + top_rows, :cut] = top_ref[:, lags - cut:]
            matrix[cut:cut + top_rows, cut:] = top_ref[:, :lags - cut]

    here = pl.multiple_of(pl.program_id(0) * group * pitch, group * pitch)
    for s in range(n_src):
        block, part = divmod(s, lag_groups)
        rows32[...] = moved_ref[s, pl.ds(here, group * pitch), :].astype(jnp.float32)
        for d in range(days_here):
            day = block * days_here + d
            for t in range(tiles):
                lane = slice(part * width + t * LANES, part * width + (t + 1) * LANES)
                x = rows32[pl.ds(t * days_here + d, group, stride=pitch), :]
                data[day, :, lane] = x
                data16[day * group:(day + 1) * group, lane] = x.astype(jnp.bfloat16)

    quad[...] = jnp.dot(data16[...], matrix[...], preferred_element_type=jnp.float32)

    scale = []
    for day in range(days):
        x = data[day]
        norm2 = jnp.sum(x * x, axis=1, keepdims=True)
        scale.append(1.0 / jnp.sqrt(norm2 / lags + epsilon))

    for c in range(0, lags, chunk):
        linear = csum = ssum = None
        for day in range(days):
            x = data[day, :, c:c + chunk]
            q = quad[day * group:(day + 1) * group, c:c + chunk]
            inv = jnp.minimum(lax.rsqrt(x * x + q * q), 10.0 * scale[day])
            xn = x * scale[day]
            data[day, :, c:c + chunk] = xn
            if day == 0:
                linear, csum, ssum = xn, x * inv, q * inv
            else:
                linear, csum, ssum = linear + xn, csum + x * inv, ssum + q * inv
        stack[:, c:c + chunk] = linear / days * ((csum * csum + ssum * ssum) / (days * days))

    bands = group // SUBLANES
    all_bands = bands * pl.num_programs(0)

    def emit(kind, value):
        peak = jnp.maximum(jnp.max(jnp.abs(value), axis=1, keepdims=True), 1e-30)
        power = jnp.floor(jnp.log2(peak))
        value = value * jnp.exp2(9.0 - power)
        for part in range(lag_groups):
            for r in range(bands):
                for t in range(tiles):
                    place = (kind * all_bands + pl.program_id(0) * bands + r) * tiles + t
                    lane = part * width + t * LANES
                    for copy in range(part, message_ref.shape[0], lag_groups):
                        message_ref[copy, place] = value[r * SUBLANES:(r + 1) * SUBLANES, lane:lane + LANES]
        return power

    powers = [emit(0, stack[...])]
    for step in range(ITERS):
        s = stack[...]
        msq = jnp.sum(s * s, axis=1, keepdims=True) / lags
        normed[...] = s * (1.0 / jnp.sqrt(msq + epsilon))
        cohs, ress = [], []
        for day in range(days):
            cohs.append(jnp.sum(data[day] * normed[...], axis=1, keepdims=True) / lags)
        for day in range(days):
            gap = data[day] - cohs[day] * normed[...]
            ress.append(jnp.sum(gap * gap, axis=1, keepdims=True) / lags)
        rbar = sum(ress[1:], ress[0]) / days
        weights = [(0.1 + jnp.abs(c)) / (r + rbar + epsilon) for c, r in zip(cohs, ress)]
        if step == ITERS - 1:
            total = sum(weights[1:], weights[0])
            weights = [w / total for w in weights]
        for c in range(0, lags, chunk):
            acc = weights[0] * data[0, :, c:c + chunk]
            for day in range(1, days):
                acc = acc + weights[day] * data[day, :, c:c + chunk]
            stack[:, c:c + chunk] = acc
    powers.append(emit(1, stack[...]))
    side = jnp.concatenate([w * 1024.0 for w in weights] + powers, axis=1)
    per = LANES // (days + 2)
    for r in range(bands):
        band = pl.program_id(0) * bands + r
        for k in range(per):
            @pl.when(band % per == k)
            def _():
                for part in range(message_ref.shape[0]):
                    message_ref[part, 2 * tiles * all_bands + band // per, :, k * (days + 2):(k + 1) * (days + 2)] = (
                        side[r * SUBLANES:(r + 1) * SUBLANES])


def stack_pairs(moved, top, lag_groups, days_here, pairs, group, n_src, repeats):
    lags = top.shape[1]
    days = n_src // lag_groups * days_here
    width = lags // lag_groups
    pitch = width // LANES * days_here
    bands = pairs // SUBLANES
    tiles = 2 * bands * (width // LANES) + pl.cdiv(bands, LANES // (days + 2))
    cost = pl.CostEstimate(
        flops=2 * pairs * days * lags * lags, bytes_accessed=pairs * days * lags * 2, transcendentals=pairs * days * lags
    )
    need = 2 * lags * lags + 10 * days * group * lags + 8 * group * lags + 2 * moved.size + 4 * top.size
    need += 4 * repeats * lag_groups * tiles * SUBLANES * LANES
    return pl.pallas_call(
        functools.partial(stack_kernel, (lag_groups, days_here, group, lags, n_src)),
        grid=(pairs // group,),
        in_specs=[pl.BlockSpec(top.shape, lambda i: (0, 0)), pl.BlockSpec(memory_space=pltpu.VMEM)],
        out_specs=pl.BlockSpec(memory_space=pltpu.VMEM),
        out_shape=jax.ShapeDtypeStruct((repeats * lag_groups, tiles, SUBLANES, LANES), jnp.float32),
        scratch_shapes=[
            pltpu.VMEM((lags, lags), jnp.bfloat16),
            pltpu.VMEM((group * pitch, LANES), jnp.float32),
            pltpu.VMEM((days, group, lags), jnp.float32),
            pltpu.VMEM((days * group, lags), jnp.bfloat16),
            pltpu.VMEM((days * group, lags), jnp.float32),
            pltpu.VMEM((group, lags), jnp.float32),
            pltpu.VMEM((group, lags), jnp.float32),
        ],
        cost_estimate=cost,
        compiler_params=pltpu.CompilerParams(vmem_limit_bytes=need + 6 * 2**20),
        name="stack_pairs",
    )(top, moved)


def place_kernel(sizes, me_ref, *refs):
    pairs, row, moves, n_old, lag_groups, days, days_here = sizes
    n_blocks = len(moves)
    blocks = refs[:n_blocks]
    outs, buffers, sems = refs[n_blocks + n_old:-4], refs[-4:-1], refs[-1]
    bands = pairs // SUBLANES
    tiles = buffers[0].shape[2] // LANES
    per = LANES // (days + 2)
    my_day = me_ref[0] // lag_groups
    copies = []
    for b, (block, move) in enumerate(zip(blocks, moves)):
        sources = block.shape[0]
        for i in range(sources):
            for group in range(pl.cdiv(bands, per)):
                side = block[i, 2 * bands * tiles + group]
                scales = jnp.exp2(side - 9.0)
                for r in range(group * per, min(bands, (group + 1) * per)):
                    lane = (r - group * per) * (days + 2)
                    at = slice((i * bands + r) * SUBLANES, (i * bands + r + 1) * SUBLANES)
                    for kind in range(2):
                        scale = jnp.broadcast_to(scales[:, lane + days + kind:lane + days + kind + 1], (SUBLANES, LANES))
                        for t in range(tiles):
                            buffers[kind][b, at, t * LANES:(t + 1) * LANES] = (
                                block[i, (kind * bands + r) * tiles + t] * scale)
                    shift = (2 * LANES - lane - my_day * days_here) % LANES
                    buffers[2][b, at, :] = pltpu.roll(side, shift, 1) * (1.0 / 1024.0)
        rows = sources * pairs
        first = row
        if move is not None:
            first = pl.multiple_of(row + (my_day ^ move) * rows, SUBLANES)
        for k in range(3):
            copy = pltpu.make_async_copy(buffers[k].at[b], outs[k].at[pl.ds(first, rows), :], sems.at[k, b])
            copy.start()
            copies.append(copy)
    for copy in copies:
        copy.wait()


def place(outs, blocks, moves, me, shapes, row, pairs, lag_groups, days, days_here):
    blocks = [b.astype(jnp.float32) for b in blocks]
    rows = blocks[0].shape[0] * pairs
    n = len(blocks)
    old = list(outs or [])
    return pl.pallas_call(
        functools.partial(place_kernel, (pairs, row, moves, len(old), lag_groups, days, days_here)),
        in_specs=[pl.BlockSpec(memory_space=pltpu.SMEM)] + [pl.BlockSpec(memory_space=pltpu.VMEM)] * n
        + [pl.BlockSpec(memory_space=pl.ANY)] * len(old),
        out_specs=[pl.BlockSpec(memory_space=pl.ANY)] * 3,
        out_shape=[jax.ShapeDtypeStruct(shape, jnp.float32) for shape in shapes],
        input_output_aliases={1 + n + k: k for k in range(len(old))},
        scratch_shapes=[pltpu.VMEM((n, rows, shape[1]), jnp.float32) for shape in shapes] + [pltpu.SemaphoreType.DMA((3, n))],
        cost_estimate=pl.CostEstimate(flops=4 * n * rows * shapes[0][1], bytes_accessed=16 * n * rows * shapes[0][1], transcendentals=0),
        compiler_params=pltpu.CompilerParams(vmem_limit_bytes=20 * 2**20),
        name="place",
    )(me.reshape(1), *blocks, *old)


AXES = ("day", "lag")


def swap(x, n, by):
    return lax.ppermute(x, AXES, [(i, i ^ by) for i in range(n)])


def unswap(pieces, index):
    step = 1
    while step < len(pieces):
        odd = (index // step) % 2 == 1
        pieces = [jnp.where(odd, pieces[k ^ step], pieces[k]) for k in range(len(pieces))]
        step *= 2
    return pieces


def spread_lags(message, me, lag_groups, n):
    lag = me % lag_groups
    pieces = unswap([message[m] for m in range(lag_groups)], lag)
    got = [pieces[0]] + [swap(pieces[m], n, m) for m in range(1, lag_groups)]
    return jnp.stack(unswap(got, lag))


def spread_days(mine, lag_groups, n):
    far = swap(mine, n, 2 * lag_groups)
    near = swap(mine, n, lag_groups)
    last = swap(far, n, lag_groups)
    return (0, 2, 1, 3), (mine, far, near, last)


def per_device(corr):
    pairs, days_here, width = corr.shape
    lag_groups = lax.axis_size("lag")
    day_groups = lax.axis_size("day")
    n = lag_groups * day_groups
    me = lax.axis_index(AXES)
    lags = width * lag_groups
    days = days_here * day_groups
    tiles = width // LANES
    top = kernel_rows(min(256, lags), lags)
    mine = pairs // n
    staged = day_groups == 4 and lag_groups == 4 and mine == sum(p for p, _, _ in PLAN)
    plan = PLAN if staged else ((mine, "all", "all"),)

    def flat(piece, lead):
        piece = piece.reshape(lead + (piece.shape[-3], days_here, tiles, LANES))
        piece = jnp.swapaxes(piece, -2, -3)
        return piece.reshape(lead + (-1, LANES))

    starts = [sum(p for p, _, _ in plan[:k]) for k in range(len(plan))]
    moved, sent = [], []

    def work(k):
        message = stack_pairs(moved[k], top, lag_groups, days_here, plan[k][0], 16 if plan[k][0] % 16 == 0 else 8, n,
                              1 if plan[k][2] == "staged" else day_groups)
        message = message.astype(jnp.float16)
        if plan[k][2] == "staged":
            message = spread_lags(message, me, lag_groups, n)
        sent.append(message)

    for k, (p, _, _) in enumerate(plan):
        if k >= 2:
            work(k - 2)
        if k == 1:
            corr, top = lax.optimization_barrier((corr, top))
        rows = corr[starts[k] * n:(starts[k] + p) * n]
        if k >= 1:
            rows, moved[k - 1] = lax.optimization_barrier((rows, moved[k - 1]))
        if k >= 2:
            rows, sent[k - 2] = lax.optimization_barrier((rows, sent[k - 2]))
        got = lax.all_to_all(rows, AXES, 0, 0, tiled=True)
        moved.append(flat(got.reshape(n, p, days_here, width), (n,)))
    for k in range(len(sent), len(plan)):
        work(k)
    shapes = ((pairs, width), (pairs, width), (pairs, LANES))
    outs = None
    todo = []
    for k, (p, _, how) in enumerate(plan):
        if how == "all":
            turns = [((None,), (lax.all_to_all(sent[k], AXES, 0, 0, tiled=True),))]
        else:
            moves, blocks = spread_days(sent[k], lag_groups, n)
            turns = [(moves[:2], blocks[:2]), (moves[2:], blocks[2:])]
        todo.append((k, turns))
    turns_of = {k: list(turns) for k, turns in todo}
    last = len(plan) - 1
    sequence = [(k, 0) for k in range(last - 1)]
    if last:
        sequence += [(k, 1) for k in range(last - 1)] + [(last - 1, 0), (last - 1, 1)]
    sequence.append((last, 0))
    for k, turn in sequence:
        moves, blocks = turns_of[k][turn]
        outs = place(outs, blocks, moves, me, shapes, starts[k] * n, plan[k][0], lag_groups, days, days_here)
    return outs[0], outs[1], outs[2][:, :days_here]


def solution(mesh):
    return jax.shard_map(
        per_device,
        mesh=mesh,
        in_specs=(P("pair", "day", "lag"),),
        out_specs=(P("pair", "lag"), P("pair", "lag"), P("pair", "day")),
        check_vma=False,
    )
```

```python
import functools

import jax
import jax.numpy as jnp
from jax import lax
from jax.experimental import pallas as pl
from jax.experimental.pallas import tpu as pltpu
from jax.sharding import PartitionSpec as P


ITERS = 3
LANES = 128
SUBLANES = 8
TOP_SPACE = pltpu.HBM
PLAN = ((16, "all", "staged"), (32, "all", "staged"), (16, "all", "all"),)
epsilon = 1e-06


def kernel_rows(rows, lags):
    row = jnp.arange(rows, dtype=jnp.int32)
    col = jnp.arange(lags, dtype=jnp.int32)
    offset = (col[None, :] - row[:, None]) % lags
    odd = offset % 2 == 1
    angle = jnp.pi * offset.astype(jnp.float32) / lags
    value = jnp.where(odd, 2.0 / lags * jnp.cos(angle) / jnp.where(odd, jnp.sin(angle), 1.0), 0.0)
    return value.astype(jnp.bfloat16)


def stack_kernel(sizes, top_hbm, moved_ref, message_ref, top_ref, top_sem, rows32, data, data16, quad, normed, stack):
    lag_groups, days_here, group, lags, n_src = sizes
    days = n_src // lag_groups * days_here
    width = lags // lag_groups
    tiles = width // LANES
    top_rows = top_ref.shape[0]
    pitch = tiles * days_here
    chunk = min(512, width)

    fetch = pltpu.make_async_copy(top_hbm, top_ref, top_sem)

    @pl.when(pl.program_id(0) == 0)
    def _():
        fetch.start()

    here = pl.multiple_of(pl.program_id(0) * group * pitch, group * pitch)
    for s in range(n_src):
        block, part = divmod(s, lag_groups)
        rows32[...] = moved_ref[s, pl.ds(here, group * pitch), :].astype(jnp.float32)
        for d in range(days_here):
            day = block * days_here + d
            for t in range(tiles):
                lane = slice(part * width + t * LANES, part * width + (t + 1) * LANES)
                x = rows32[pl.ds(t * days_here + d, group, stride=pitch), :]
                data[day, :, lane] = x
                data16[day * group:(day + 1) * group, lane] = x.astype(jnp.bfloat16)

    @pl.when(pl.program_id(0) == 0)
    def _():
        fetch.wait()

    bands_of_matrix = [top_ref[...]]
    for cut in range(top_rows, lags, top_rows):
        bands_of_matrix.append(jnp.concatenate([top_ref[:, lags - cut:], top_ref[:, :lags - cut]], axis=1))
    quad[...] = jnp.dot(data16[...], jnp.concatenate(bands_of_matrix, axis=0), preferred_element_type=jnp.float32)

    scale = []
    for day in range(days):
        x = data[day]
        norm2 = jnp.sum(x * x, axis=1, keepdims=True)
        scale.append(1.0 / jnp.sqrt(norm2 / lags + epsilon))

    for c in range(0, lags, chunk):
        linear = csum = ssum = None
        for day in range(days):
            x = data[day, :, c:c + chunk]
            q = quad[day * group:(day + 1) * group, c:c + chunk]
            inv = jnp.minimum(lax.rsqrt(x * x + q * q), 10.0 * scale[day])
            xn = x * scale[day]
            data[day, :, c:c + chunk] = xn
            if day == 0:
                linear, csum, ssum = xn, x * inv, q * inv
            else:
                linear, csum, ssum = linear + xn, csum + x * inv, ssum + q * inv
        stack[:, c:c + chunk] = linear / days * ((csum * csum + ssum * ssum) / (days * days))

    bands = group // SUBLANES
    all_bands = bands * pl.num_programs(0)

    def emit(kind, value):
        peak = jnp.maximum(jnp.max(jnp.abs(value), axis=1, keepdims=True), 1e-30)
        power = jnp.floor(jnp.log2(peak))
        value = value * jnp.exp2(9.0 - power)
        for part in range(lag_groups):
            for r in range(bands):
                for t in range(tiles):
                    place = (kind * all_bands + pl.program_id(0) * bands + r) * tiles + t
                    lane = part * width + t * LANES
                    for copy in range(part, message_ref.shape[0], lag_groups):
                        message_ref[copy, place] = value[r * SUBLANES:(r + 1) * SUBLANES, lane:lane + LANES]
        return power

    powers = [emit(0, stack[...])]
    for step in range(ITERS):
        s = stack[...]
        msq = jnp.sum(s * s, axis=1, keepdims=True) / lags
        normed[...] = s * (1.0 / jnp.sqrt(msq + epsilon))
        cohs, ress = [], []
        for day in range(days):
            cohs.append(jnp.sum(data[day] * normed[...], axis=1, keepdims=True) / lags)
        for day in range(days):
            gap = data[day] - cohs[day] * normed[...]
            ress.append(jnp.sum(gap * gap, axis=1, keepdims=True) / lags)
        rbar = sum(ress[1:], ress[0]) / days
        weights = [(0.1 + jnp.abs(c)) / (r + rbar + epsilon) for c, r in zip(cohs, ress)]
        if step == ITERS - 1:
            total = sum(weights[1:], weights[0])
            weights = [w / total for w in weights]
        for c in range(0, lags, chunk):
            acc = weights[0] * data[0, :, c:c + chunk]
            for day in range(1, days):
                acc = acc + weights[day] * data[day, :, c:c + chunk]
            stack[:, c:c + chunk] = acc
    powers.append(emit(1, stack[...]))
    side = jnp.concatenate([w * 1024.0 for w in weights] + powers, axis=1)
    per = LANES // (days + 2)
    for r in range(bands):
        band = pl.program_id(0) * bands + r
        for k in range(per):
            @pl.when(band % per == k)
            def _():
                for part in range(message_ref.shape[0]):
                    message_ref[part, 2 * tiles * all_bands + band // per, :, k * (days + 2):(k + 1) * (days + 2)] = (
                        side[r * SUBLANES:(r + 1) * SUBLANES])


def stack_pairs(moved, top, lag_groups, days_here, pairs, group, n_src, repeats):
    lags = top.shape[1]
    days = n_src // lag_groups * days_here
    width = lags // lag_groups
    pitch = width // LANES * days_here
    bands = pairs // SUBLANES
    tiles = 2 * bands * (width // LANES) + pl.cdiv(bands, LANES // (days + 2))
    cost = pl.CostEstimate(
        flops=2 * pairs * days * lags * lags, bytes_accessed=pairs * days * lags * 2, transcendentals=pairs * days * lags
    )
    need = 10 * days * group * lags + 8 * group * lags + 2 * moved.size + 4 * top.size
    need += 4 * repeats * lag_groups * tiles * SUBLANES * LANES
    return pl.pallas_call(
        functools.partial(stack_kernel, (lag_groups, days_here, group, lags, n_src)),
        grid=(pairs // group,),
        in_specs=[pl.BlockSpec(memory_space=TOP_SPACE), pl.BlockSpec(memory_space=pltpu.VMEM)],
        out_specs=pl.BlockSpec(memory_space=pltpu.VMEM),
        out_shape=jax.ShapeDtypeStruct((repeats * lag_groups, tiles, SUBLANES, LANES), jnp.float32),
        scratch_shapes=[
            pltpu.VMEM(top.shape, top.dtype),
            pltpu.SemaphoreType.DMA,
            pltpu.VMEM((group * pitch, LANES), jnp.float32),
            pltpu.VMEM((days, group, lags), jnp.float32),
            pltpu.VMEM((days * group, lags), jnp.bfloat16),
            pltpu.VMEM((days * group, lags), jnp.float32),
            pltpu.VMEM((group, lags), jnp.float32),
            pltpu.VMEM((group, lags), jnp.float32),
        ],
        cost_estimate=cost,
        compiler_params=pltpu.CompilerParams(vmem_limit_bytes=need + 6 * 2**20),
        name="stack_pairs",
    )(pltpu.with_memory_space_constraint(top, pltpu.HBM), moved)


def place_kernel(sizes, me_ref, *refs):
    pairs, row, moves, n_old, lag_groups, days, days_here = sizes
    n_blocks = len(moves)
    blocks = refs[:n_blocks]
    outs, buffers, sems = refs[n_blocks + n_old:-4], refs[-4:-1], refs[-1]
    bands = pairs // SUBLANES
    tiles = buffers[0].shape[2] // LANES
    per = LANES // (days + 2)
    my_day = me_ref[0] // lag_groups
    copies = []
    for b, (block, move) in enumerate(zip(blocks, moves)):
        sources = block.shape[0]
        for i in range(sources):
            for group in range(pl.cdiv(bands, per)):
                side = block[i, 2 * bands * tiles + group]
                scales = jnp.exp2(side - 9.0)
                for r in range(group * per, min(bands, (group + 1) * per)):
                    lane = (r - group * per) * (days + 2)
                    at = slice((i * bands + r) * SUBLANES, (i * bands + r + 1) * SUBLANES)
                    for kind in range(2):
                        scale = jnp.broadcast_to(scales[:, lane + days + kind:lane + days + kind + 1], (SUBLANES, LANES))
                        for t in range(tiles):
                            buffers[kind][b, at, t * LANES:(t + 1) * LANES] = (
                                block[i, (kind * bands + r) * tiles + t] * scale)
                    shift = (2 * LANES - lane - my_day * days_here) % LANES
                    buffers[2][b, at, :] = pltpu.roll(side, shift, 1) * (1.0 / 1024.0)
        rows = sources * pairs
        first = row
        if move is not None:
            first = pl.multiple_of(row + (my_day ^ move) * rows, SUBLANES)
        for k in range(3):
            copy = pltpu.make_async_copy(buffers[k].at[b], outs[k].at[pl.ds(first, rows), :], sems.at[k, b])
            copy.start()
            copies.append(copy)
    for copy in copies:
        copy.wait()


def place(outs, blocks, moves, me, shapes, row, pairs, lag_groups, days, days_here):
    blocks = [b.astype(jnp.float32) for b in blocks]
    rows = blocks[0].shape[0] * pairs
    n = len(blocks)
    old = list(outs or [])
    return pl.pallas_call(
        functools.partial(place_kernel, (pairs, row, moves, len(old), lag_groups, days, days_here)),
        in_specs=[pl.BlockSpec(memory_space=pltpu.SMEM)] + [pl.BlockSpec(memory_space=pltpu.VMEM)] * n
        + [pl.BlockSpec(memory_space=pl.ANY)] * len(old),
        out_specs=[pl.BlockSpec(memory_space=pl.ANY)] * 3,
        out_shape=[jax.ShapeDtypeStruct(shape, jnp.float32) for shape in shapes],
        input_output_aliases={1 + n + k: k for k in range(len(old))},
        scratch_shapes=[pltpu.VMEM((n, rows, shape[1]), jnp.float32) for shape in shapes] + [pltpu.SemaphoreType.DMA((3, n))],
        cost_estimate=pl.CostEstimate(flops=4 * n * rows * shapes[0][1], bytes_accessed=16 * n * rows * shapes[0][1], transcendentals=0),
        compiler_params=pltpu.CompilerParams(vmem_limit_bytes=20 * 2**20),
        name="place",
    )(me.reshape(1), *blocks, *old)


AXES = ("day", "lag")


def swap(x, n, by):
    return lax.ppermute(x, AXES, [(i, i ^ by) for i in range(n)])


def unswap(pieces, index):
    step = 1
    while step < len(pieces):
        odd = (index // step) % 2 == 1
        pieces = [jnp.where(odd, pieces[k ^ step], pieces[k]) for k in range(len(pieces))]
        step *= 2
    return pieces


def spread_lags(message, me, lag_groups, n):
    lag = me % lag_groups
    pieces = unswap([message[m] for m in range(lag_groups)], lag)
    got = [pieces[0]] + [swap(pieces[m], n, m) for m in range(1, lag_groups)]
    return jnp.stack(unswap(got, lag))


def spread_days(mine, lag_groups, n):
    far = swap(mine, n, 2 * lag_groups)
    near = swap(mine, n, lag_groups)
    last = swap(far, n, lag_groups)
    return (0, 2, 1, 3), (mine, far, near, last)


def per_device(corr):
    pairs, days_here, width = corr.shape
    lag_groups = lax.axis_size("lag")
    day_groups = lax.axis_size("day")
    n = lag_groups * day_groups
    me = lax.axis_index(AXES)
    lags = width * lag_groups
    days = days_here * day_groups
    tiles = width // LANES
    top = kernel_rows(min(256, lags), lags)
    mine = pairs // n
    staged = day_groups == 4 and lag_groups == 4 and mine == sum(p for p, _, _ in PLAN)
    plan = PLAN if staged else ((mine, "all", "all"),)

    def flat(piece, lead):
        piece = piece.reshape(lead + (piece.shape[-3], days_here, tiles, LANES))
        piece = jnp.swapaxes(piece, -2, -3)
        return piece.reshape(lead + (-1, LANES))

    starts = [sum(p for p, _, _ in plan[:k]) for k in range(len(plan))]
    moved, sent = [], []

    def work(k):
        message = stack_pairs(moved[k], top, lag_groups, days_here, plan[k][0], plan[k][0] if plan[k][0] <= 32 else (16 if plan[k][0] % 16 == 0 else 8), n,
                              1 if plan[k][2] == "staged" else day_groups)
        message = message.astype(jnp.float16)
        if plan[k][2] == "staged":
            message = spread_lags(message, me, lag_groups, n)
        sent.append(message)

    for k, (p, _, _) in enumerate(plan):
        if k >= 2:
            work(k - 2)
        if k == 1:
            corr, top = lax.optimization_barrier((corr, top))
        rows = corr[starts[k] * n:(starts[k] + p) * n]
        if k >= 1:
            rows, moved[k - 1] = lax.optimization_barrier((rows, moved[k - 1]))
        if k >= 2:
            rows, sent[k - 2] = lax.optimization_barrier((rows, sent[k - 2]))
        got = lax.all_to_all(rows, AXES, 0, 0, tiled=True)
        moved.append(flat(got.reshape(n, p, days_here, width), (n,)))
    for k in range(len(sent), len(plan)):
        work(k)
    shapes = ((pairs, width), (pairs, width), (pairs, LANES))
    outs = None
    todo = []
    for k, (p, _, how) in enumerate(plan):
        if how == "all":
            turns = [((None,), (lax.all_to_all(sent[k], AXES, 0, 0, tiled=True),))]
        else:
            moves, blocks = spread_days(sent[k], lag_groups, n)
            turns = [(moves[:2], blocks[:2]), (moves[2:], blocks[2:])]
        todo.append((k, turns))
    turns_of = {k: list(turns) for k, turns in todo}
    last = len(plan) - 1
    sequence = [(k, 0) for k in range(last - 1)]
    if last:
        sequence += [(k, 1) for k in range(last - 1)] + [(last - 1, 0), (last - 1, 1)]
    sequence.append((last, 0))
    for k, turn in sequence:
        moves, blocks = turns_of[k][turn]
        outs = place(outs, blocks, moves, me, shapes, starts[k] * n, plan[k][0], lag_groups, days, days_here)
    return outs[0], outs[1], outs[2][:, :days_here]


def solution(mesh):
    return jax.shard_map(
        per_device,
        mesh=mesh,
        in_specs=(P("pair", "day", "lag"),),
        out_specs=(P("pair", "lag"), P("pair", "lag"), P("pair", "day")),
        check_vma=False,
    )
```

```python
import functools

import jax
import jax.numpy as jnp
from jax import lax
from jax.experimental import pallas as pl
from jax.experimental.pallas import tpu as pltpu
from jax.sharding import PartitionSpec as P


ITERS = 3
LANES = 128
SUBLANES = 8
TOP_SPACE = pltpu.HBM
PLAN = ((32, "all", "staged"), (16, "swap", "staged"), (16, "all", "all"))
epsilon = 1e-06


def kernel_rows(rows, lags):
    row = jnp.arange(rows, dtype=jnp.int32)
    col = jnp.arange(lags, dtype=jnp.int32)
    offset = (col[None, :] - row[:, None]) % lags
    odd = offset % 2 == 1
    angle = jnp.pi * offset.astype(jnp.float32) / lags
    value = jnp.where(odd, 2.0 / lags * jnp.cos(angle) / jnp.where(odd, jnp.sin(angle), 1.0), 0.0)
    return value.astype(jnp.bfloat16)


def stack_kernel(sizes, me_ref, top_hbm, *refs):
    lag_groups, days_here, group, lags, n_src = sizes
    ins = refs[:-9]
    message_ref, top_ref, top_sem, rows32, data, data16, quad, normed, stack = refs[-9:]
    days = n_src // lag_groups * days_here
    width = lags // lag_groups
    tiles = width // LANES
    top_rows = top_ref.shape[0]
    pitch = tiles * days_here
    chunk = min(512, width)

    fetch = pltpu.make_async_copy(top_hbm, top_ref, top_sem)

    @pl.when(pl.program_id(0) == 0)
    def _():
        fetch.start()

    here = pl.multiple_of(pl.program_id(0) * group * pitch, group * pitch)
    for s in range(n_src):
        if len(ins) == 1:
            rows32[...] = ins[0][s, pl.ds(here, group * pitch), :].astype(jnp.float32)
            block, part = divmod(s, lag_groups)
        else:
            rows32[...] = ins[s][pl.ds(here, group * pitch), :].astype(jnp.float32)
            source = me_ref[0] ^ s
            block, part = source // lag_groups, source % lag_groups
        for d in range(days_here):
            day = block * days_here + d
            row = pl.multiple_of(day * group, group)
            for t in range(tiles):
                lane = pl.ds(pl.multiple_of(part * width + t * LANES, LANES), LANES)
                x = rows32[pl.ds(t * days_here + d, group, stride=pitch), :]
                data[day, :, lane] = x
                data16[pl.ds(row, group), lane] = x.astype(jnp.bfloat16)

    @pl.when(pl.program_id(0) == 0)
    def _():
        fetch.wait()

    bands_of_matrix = [top_ref[...]]
    for cut in range(top_rows, lags, top_rows):
        bands_of_matrix.append(jnp.concatenate([top_ref[:, lags - cut:], top_ref[:, :lags - cut]], axis=1))
    quad[...] = jnp.dot(data16[...], jnp.concatenate(bands_of_matrix, axis=0), preferred_element_type=jnp.float32)

    scale = []
    for day in range(days):
        x = data[day]
        norm2 = jnp.sum(x * x, axis=1, keepdims=True)
        scale.append(1.0 / jnp.sqrt(norm2 / lags + epsilon))

    for c in range(0, lags, chunk):
        linear = csum = ssum = None
        for day in range(days):
            x = data[day, :, c:c + chunk]
            q = quad[day * group:(day + 1) * group, c:c + chunk]
            inv = jnp.minimum(lax.rsqrt(x * x + q * q), 10.0 * scale[day])
            xn = x * scale[day]
            data[day, :, c:c + chunk] = xn
            if day == 0:
                linear, csum, ssum = xn, x * inv, q * inv
            else:
                linear, csum, ssum = linear + xn, csum + x * inv, ssum + q * inv
        stack[:, c:c + chunk] = linear / days * ((csum * csum + ssum * ssum) / (days * days))

    bands = group // SUBLANES
    all_bands = bands * pl.num_programs(0)

    def emit(kind, value):
        peak = jnp.maximum(jnp.max(jnp.abs(value), axis=1, keepdims=True), 1e-30)
        power = jnp.floor(jnp.log2(peak))
        value = value * jnp.exp2(9.0 - power)
        for part in range(lag_groups):
            for r in range(bands):
                for t in range(tiles):
                    place = (kind * all_bands + pl.program_id(0) * bands + r) * tiles + t
                    lane = part * width + t * LANES
                    for copy in range(part, message_ref.shape[0], lag_groups):
                        message_ref[copy, place] = value[r * SUBLANES:(r + 1) * SUBLANES, lane:lane + LANES]
        return power

    powers = [emit(0, stack[...])]
    for step in range(ITERS):
        s = stack[...]
        msq = jnp.sum(s * s, axis=1, keepdims=True) / lags
        normed[...] = s * (1.0 / jnp.sqrt(msq + epsilon))
        cohs, ress = [], []
        for day in range(days):
            cohs.append(jnp.sum(data[day] * normed[...], axis=1, keepdims=True) / lags)
        for day in range(days):
            gap = data[day] - cohs[day] * normed[...]
            ress.append(jnp.sum(gap * gap, axis=1, keepdims=True) / lags)
        rbar = sum(ress[1:], ress[0]) / days
        weights = [(0.1 + jnp.abs(c)) / (r + rbar + epsilon) for c, r in zip(cohs, ress)]
        if step == ITERS - 1:
            total = sum(weights[1:], weights[0])
            weights = [w / total for w in weights]
        for c in range(0, lags, chunk):
            acc = weights[0] * data[0, :, c:c + chunk]
            for day in range(1, days):
                acc = acc + weights[day] * data[day, :, c:c + chunk]
            stack[:, c:c + chunk] = acc
    powers.append(emit(1, stack[...]))
    side = jnp.concatenate([w * 1024.0 for w in weights] + powers, axis=1)
    per = LANES // (days + 2)
    for r in range(bands):
        band = pl.program_id(0) * bands + r
        for k in range(per):
            @pl.when(band % per == k)
            def _():
                for part in range(message_ref.shape[0]):
                    message_ref[part, 2 * tiles * all_bands + band // per, :, k * (days + 2):(k + 1) * (days + 2)] = (
                        side[r * SUBLANES:(r + 1) * SUBLANES])


def stack_pairs(me, moved, top, lag_groups, days_here, pairs, group, n_src, repeats):
    lags = top.shape[1]
    days = n_src // lag_groups * days_here
    width = lags // lag_groups
    pitch = width // LANES * days_here
    bands = pairs // SUBLANES
    tiles = 2 * bands * (width // LANES) + pl.cdiv(bands, LANES // (days + 2))
    cost = pl.CostEstimate(
        flops=2 * pairs * days * lags * lags, bytes_accessed=pairs * days * lags * 2, transcendentals=pairs * days * lags
    )
    need = 10 * days * group * lags + 8 * group * lags + 2 * sum(m.size for m in moved) + 4 * top.size
    need += 4 * repeats * lag_groups * tiles * SUBLANES * LANES
    return pl.pallas_call(
        functools.partial(stack_kernel, (lag_groups, days_here, group, lags, n_src)),
        grid=(pairs // group,),
        in_specs=[pl.BlockSpec(memory_space=pltpu.SMEM), pl.BlockSpec(memory_space=TOP_SPACE)]
        + [pl.BlockSpec(memory_space=pltpu.VMEM)] * len(moved),
        out_specs=pl.BlockSpec(memory_space=pltpu.VMEM),
        out_shape=jax.ShapeDtypeStruct((repeats * lag_groups, tiles, SUBLANES, LANES), jnp.float32),
        scratch_shapes=[
            pltpu.VMEM(top.shape, top.dtype),
            pltpu.SemaphoreType.DMA,
            pltpu.VMEM((group * pitch, LANES), jnp.float32),
            pltpu.VMEM((days, group, lags), jnp.float32),
            pltpu.VMEM((days * group, lags), jnp.bfloat16),
            pltpu.VMEM((days * group, lags), jnp.float32),
            pltpu.VMEM((group, lags), jnp.float32),
            pltpu.VMEM((group, lags), jnp.float32),
        ],
        cost_estimate=cost,
        compiler_params=pltpu.CompilerParams(vmem_limit_bytes=need + 6 * 2**20),
        name="stack_pairs",
    )(me.reshape(1), pltpu.with_memory_space_constraint(top, pltpu.HBM), *moved)


def place_kernel(sizes, me_ref, *refs):
    pairs, row, moves, n_old, lag_groups, days, days_here = sizes
    n_blocks = len(moves)
    blocks = refs[:n_blocks]
    outs, buffers, sems = refs[n_blocks + n_old:-4], refs[-4:-1], refs[-1]
    bands = pairs // SUBLANES
    tiles = buffers[0].shape[2] // LANES
    per = LANES // (days + 2)
    my_day = me_ref[0] // lag_groups
    copies = []
    for b, (block, move) in enumerate(zip(blocks, moves)):
        sources = block.shape[0]
        for i in range(sources):
            for group in range(pl.cdiv(bands, per)):
                side = block[i, 2 * bands * tiles + group]
                scales = jnp.exp2(side - 9.0)
                for r in range(group * per, min(bands, (group + 1) * per)):
                    lane = (r - group * per) * (days + 2)
                    at = slice((i * bands + r) * SUBLANES, (i * bands + r + 1) * SUBLANES)
                    for kind in range(2):
                        scale = jnp.broadcast_to(scales[:, lane + days + kind:lane + days + kind + 1], (SUBLANES, LANES))
                        for t in range(tiles):
                            buffers[kind][b, at, t * LANES:(t + 1) * LANES] = (
                                block[i, (kind * bands + r) * tiles + t] * scale)
                    shift = (2 * LANES - lane - my_day * days_here) % LANES
                    buffers[2][b, at, :] = pltpu.roll(side, shift, 1) * (1.0 / 1024.0)
        rows = sources * pairs
        first = row
        if move is not None:
            first = pl.multiple_of(row + (my_day ^ move) * rows, SUBLANES)
        for k in range(3):
            copy = pltpu.make_async_copy(buffers[k].at[b], outs[k].at[pl.ds(first, rows), :], sems.at[k, b])
            copy.start()
            copies.append(copy)
    for copy in copies:
        copy.wait()


def place(outs, blocks, moves, me, shapes, row, pairs, lag_groups, days, days_here):
    blocks = [b.astype(jnp.float32) for b in blocks]
    rows = blocks[0].shape[0] * pairs
    n = len(blocks)
    old = list(outs or [])
    return pl.pallas_call(
        functools.partial(place_kernel, (pairs, row, moves, len(old), lag_groups, days, days_here)),
        in_specs=[pl.BlockSpec(memory_space=pltpu.SMEM)] + [pl.BlockSpec(memory_space=pltpu.VMEM)] * n
        + [pl.BlockSpec(memory_space=pl.ANY)] * len(old),
        out_specs=[pl.BlockSpec(memory_space=pl.ANY)] * 3,
        out_shape=[jax.ShapeDtypeStruct(shape, jnp.float32) for shape in shapes],
        input_output_aliases={1 + n + k: k for k in range(len(old))},
        scratch_shapes=[pltpu.VMEM((n, rows, shape[1]), jnp.float32) for shape in shapes] + [pltpu.SemaphoreType.DMA((3, n))],
        cost_estimate=pl.CostEstimate(flops=4 * n * rows * shapes[0][1], bytes_accessed=16 * n * rows * shapes[0][1], transcendentals=0),
        compiler_params=pltpu.CompilerParams(vmem_limit_bytes=20 * 2**20),
        name="place",
    )(me.reshape(1), *blocks, *old)


AXES = ("day", "lag")


def swap(x, n, by):
    return lax.ppermute(x, AXES, [(i, i ^ by) for i in range(n)])


def unswap(pieces, index):
    step = 1
    while step < len(pieces):
        odd = (index // step) % 2 == 1
        pieces = [jnp.where(odd, pieces[k ^ step], pieces[k]) for k in range(len(pieces))]
        step *= 2
    return pieces


def spread_lags(message, me, lag_groups, n):
    lag = me % lag_groups
    pieces = unswap([message[m] for m in range(lag_groups)], lag)
    got = [pieces[0]] + [swap(pieces[m], n, m) for m in range(1, lag_groups)]
    return jnp.stack(unswap(got, lag))


def spread_days(mine, lag_groups, n):
    far = swap(mine, n, 2 * lag_groups)
    near = swap(mine, n, lag_groups)
    last = swap(far, n, lag_groups)
    return (0, 2, 1, 3), (mine, far, near, last)


def per_device(corr):
    pairs, days_here, width = corr.shape
    lag_groups = lax.axis_size("lag")
    day_groups = lax.axis_size("day")
    n = lag_groups * day_groups
    me = lax.axis_index(AXES)
    lags = width * lag_groups
    days = days_here * day_groups
    tiles = width // LANES
    top = kernel_rows(min(256, lags), lags)
    mine = pairs // n
    staged = day_groups == 4 and lag_groups == 4 and mine == sum(p for p, _, _ in PLAN)
    plan = PLAN if staged else ((mine, "all", "all"),)

    def flat(piece, lead):
        piece = piece.reshape(lead + (piece.shape[-3], days_here, tiles, LANES))
        piece = jnp.swapaxes(piece, -2, -3)
        return piece.reshape(lead + (-1, LANES))

    starts = [sum(p for p, _, _ in plan[:k]) for k in range(len(plan))]
    moved, sent = [], []

    def work(k):
        message = stack_pairs(me, moved[k], top, lag_groups, days_here, plan[k][0], plan[k][0] if plan[k][0] <= 32 else (16 if plan[k][0] % 16 == 0 else 8), n,
                              1 if plan[k][2] == "staged" else day_groups)
        message = message.astype(jnp.float16)
        if plan[k][2] == "staged":
            message = spread_lags(message, me, lag_groups, n)
        sent.append(message)

    for k, (p, how, _) in enumerate(plan):
        if k == 1:
            corr, top = lax.optimization_barrier((corr, top))
        rows = corr[starts[k] * n:(starts[k] + p) * n]
        if how == "swap":
            pieces = [lax.dynamic_slice_in_dim(rows, (me ^ s) * p, p, 0) for s in range(n)]
            pieces = [pieces[0]] + [swap(pieces[s], n, s) for s in range(1, n)]
            moved.append([flat(piece, ()) for piece in pieces])
            continue
        if k >= 1:
            rows, moved[0] = lax.optimization_barrier((rows, moved[0]))
        got = lax.all_to_all(rows, AXES, 0, 0, tiled=True)
        moved.append([flat(got.reshape(n, p, days_here, width), (n,))])
    for k in range(len(sent), len(plan)):
        work(k)
    shapes = ((pairs, width), (pairs, width), (pairs, LANES))
    outs = None
    todo = []
    for k, (p, _, how) in enumerate(plan):
        if how == "all":
            turns = [((None,), (lax.all_to_all(sent[k], AXES, 0, 0, tiled=True),))]
        else:
            moves, blocks = spread_days(sent[k], lag_groups, n)
            turns = [(moves[:3], blocks[:3]), (moves[3:], blocks[3:])]
        todo.append((k, turns))
    turns_of = {k: list(turns) for k, turns in todo}
    last = len(plan) - 1
    sequence = [(k, 0) for k in range(last)] + [(k, 1) for k in range(last)] + [(last, 0)]
    for k, turn in sequence:
        moves, blocks = turns_of[k][turn]
        outs = place(outs, blocks, moves, me, shapes, starts[k] * n, plan[k][0], lag_groups, days, days_here)
    return outs[0], outs[1], outs[2][:, :days_here]


def solution(mesh):
    return jax.shard_map(
        per_device,
        mesh=mesh,
        in_specs=(P("pair", "day", "lag"),),
        out_specs=(P("pair", "lag"), P("pair", "lag"), P("pair", "day")),
        check_vma=False,
    )
```

```python
import functools

import jax
import jax.numpy as jnp
from jax import lax
from jax.experimental import pallas as pl
from jax.experimental.pallas import tpu as pltpu
from jax.sharding import PartitionSpec as P


ITERS = 3
LANES = 128
SUBLANES = 8
TOP_SPACE = pltpu.HBM
PLAN = ((32, "all", "staged"), (16, "swap", "staged"), (16, "all", "all"))
epsilon = 1e-06


def kernel_rows(rows, lags):
    row = jnp.arange(rows, dtype=jnp.int32)
    col = jnp.arange(lags, dtype=jnp.int32)
    offset = (col[None, :] - row[:, None]) % lags
    odd = offset % 2 == 1
    angle = jnp.pi * offset.astype(jnp.float32) / lags
    value = jnp.where(odd, 2.0 / lags * jnp.cos(angle) / jnp.where(odd, jnp.sin(angle), 1.0), 0.0)
    return value.astype(jnp.bfloat16)


def stack_kernel(sizes, me_ref, top_hbm, *refs):
    lag_groups, days_here, group, lags, n_src = sizes
    ins = refs[:-9]
    message_ref, top_ref, top_sem, rows32, data, data16, quad, normed, stack = refs[-9:]
    days = n_src // lag_groups * days_here
    width = lags // lag_groups
    tiles = width // LANES
    top_rows = top_ref.shape[0]
    pitch = tiles * days_here
    chunk = min(512, width)

    fetch = pltpu.make_async_copy(top_hbm, top_ref, top_sem)

    @pl.when(pl.program_id(0) == 0)
    def _():
        fetch.start()

    here = pl.multiple_of(pl.program_id(0) * group * pitch, group * pitch)
    for s in range(n_src):
        if len(ins) == 1:
            rows32[...] = ins[0][s, pl.ds(here, group * pitch), :].astype(jnp.float32)
            block, part = divmod(s, lag_groups)
        else:
            rows32[...] = ins[s][pl.ds(here, group * pitch), :].astype(jnp.float32)
            source = me_ref[0] ^ s
            block, part = source // lag_groups, source % lag_groups
        for d in range(days_here):
            day = block * days_here + d
            row = pl.multiple_of(day * group, group)
            for t in range(tiles):
                lane = pl.ds(pl.multiple_of(part * width + t * LANES, LANES), LANES)
                x = rows32[pl.ds(t * days_here + d, group, stride=pitch), :]
                data[day, :, lane] = x
                data16[pl.ds(row, group), lane] = x.astype(jnp.bfloat16)

    @pl.when(pl.program_id(0) == 0)
    def _():
        fetch.wait()

    bands_of_matrix = [top_ref[...]]
    for cut in range(top_rows, lags, top_rows):
        bands_of_matrix.append(jnp.concatenate([top_ref[:, lags - cut:], top_ref[:, :lags - cut]], axis=1))
    quad[...] = jnp.dot(data16[...], jnp.concatenate(bands_of_matrix, axis=0), preferred_element_type=jnp.float32)

    scale = []
    for day in range(days):
        x = data[day]
        norm2 = jnp.sum(x * x, axis=1, keepdims=True)
        scale.append(1.0 / jnp.sqrt(norm2 / lags + epsilon))

    for c in range(0, lags, chunk):
        linear = csum = ssum = None
        for day in range(days):
            x = data[day, :, c:c + chunk]
            q = quad[day * group:(day + 1) * group, c:c + chunk]
            inv = jnp.minimum(lax.rsqrt(x * x + q * q), 10.0 * scale[day])
            xn = x * scale[day]
            data[day, :, c:c + chunk] = xn
            if day == 0:
                linear, csum, ssum = xn, x * inv, q * inv
            else:
                linear, csum, ssum = linear + xn, csum + x * inv, ssum + q * inv
        stack[:, c:c + chunk] = linear / days * ((csum * csum + ssum * ssum) / (days * days))

    bands = group // SUBLANES
    all_bands = bands * pl.num_programs(0)

    def emit(kind, value):
        peak = jnp.maximum(jnp.max(jnp.abs(value), axis=1, keepdims=True), 1e-30)
        power = jnp.floor(jnp.log2(peak))
        value = value * jnp.exp2(9.0 - power)
        for part in range(lag_groups):
            for r in range(bands):
                for t in range(tiles):
                    place = (kind * all_bands + pl.program_id(0) * bands + r) * tiles + t
                    lane = part * width + t * LANES
                    for copy in range(part, message_ref.shape[0], lag_groups):
                        message_ref[copy, place] = value[r * SUBLANES:(r + 1) * SUBLANES, lane:lane + LANES]
        return power

    powers = [emit(0, stack[...])]
    for step in range(ITERS):
        s = stack[...]
        msq = jnp.sum(s * s, axis=1, keepdims=True) / lags
        normed[...] = s * (1.0 / jnp.sqrt(msq + epsilon))
        cohs, ress = [], []
        for day in range(days):
            cohs.append(jnp.sum(data[day] * normed[...], axis=1, keepdims=True) / lags)
        for day in range(days):
            gap = data[day] - cohs[day] * normed[...]
            ress.append(jnp.sum(gap * gap, axis=1, keepdims=True) / lags)
        rbar = sum(ress[1:], ress[0]) / days
        weights = [(0.1 + jnp.abs(c)) / (r + rbar + epsilon) for c, r in zip(cohs, ress)]
        if step == ITERS - 1:
            total = sum(weights[1:], weights[0])
            weights = [w / total for w in weights]
        for c in range(0, lags, chunk):
            acc = weights[0] * data[0, :, c:c + chunk]
            for day in range(1, days):
                acc = acc + weights[day] * data[day, :, c:c + chunk]
            stack[:, c:c + chunk] = acc
    powers.append(emit(1, stack[...]))
    side = jnp.concatenate([w * 1024.0 for w in weights] + powers, axis=1)
    per = LANES // (days + 2)
    for r in range(bands):
        band = pl.program_id(0) * bands + r
        for k in range(per):
            @pl.when(band % per == k)
            def _():
                for part in range(message_ref.shape[0]):
                    message_ref[part, 2 * tiles * all_bands + band // per, :, k * (days + 2):(k + 1) * (days + 2)] = (
                        side[r * SUBLANES:(r + 1) * SUBLANES])


def stack_pairs(me, moved, top, lag_groups, days_here, pairs, group, n_src, repeats):
    lags = top.shape[1]
    days = n_src // lag_groups * days_here
    width = lags // lag_groups
    pitch = width // LANES * days_here
    bands = pairs // SUBLANES
    tiles = 2 * bands * (width // LANES) + pl.cdiv(bands, LANES // (days + 2))
    cost = pl.CostEstimate(
        flops=2 * pairs * days * lags * lags, bytes_accessed=pairs * days * lags * 2, transcendentals=pairs * days * lags
    )
    need = 10 * days * group * lags + 8 * group * lags + 2 * sum(m.size for m in moved) + 4 * top.size
    need += 4 * repeats * lag_groups * tiles * SUBLANES * LANES
    return pl.pallas_call(
        functools.partial(stack_kernel, (lag_groups, days_here, group, lags, n_src)),
        grid=(pairs // group,),
        in_specs=[pl.BlockSpec(memory_space=pltpu.SMEM), pl.BlockSpec(memory_space=TOP_SPACE)]
        + [pl.BlockSpec(memory_space=pltpu.VMEM)] * len(moved),
        out_specs=pl.BlockSpec(memory_space=pltpu.VMEM),
        out_shape=jax.ShapeDtypeStruct((repeats * lag_groups, tiles, SUBLANES, LANES), jnp.float32),
        scratch_shapes=[
            pltpu.VMEM(top.shape, top.dtype),
            pltpu.SemaphoreType.DMA,
            pltpu.VMEM((group * pitch, LANES), jnp.float32),
            pltpu.VMEM((days, group, lags), jnp.float32),
            pltpu.VMEM((days * group, lags), jnp.bfloat16),
            pltpu.VMEM((days * group, lags), jnp.float32),
            pltpu.VMEM((group, lags), jnp.float32),
            pltpu.VMEM((group, lags), jnp.float32),
        ],
        cost_estimate=cost,
        compiler_params=pltpu.CompilerParams(vmem_limit_bytes=need + 6 * 2**20),
        name="stack_pairs",
    )(me.reshape(1), pltpu.with_memory_space_constraint(top, pltpu.HBM), *moved)


def take_kernel(corr_ref, out_ref, sems):
    parts = sems.shape[0]
    step = out_ref.shape[0] // parts
    copies = [
        pltpu.make_async_copy(corr_ref.at[pl.ds(k * step, step)], out_ref.at[pl.ds(k * step, step)], sems.at[k])
        for k in range(parts)
    ]
    for copy in copies:
        copy.start()
    for copy in copies:
        copy.wait()


def take(corr, rows):
    return pl.pallas_call(
        take_kernel,
        in_specs=[pl.BlockSpec(memory_space=pltpu.HBM)],
        out_specs=pl.BlockSpec(memory_space=pltpu.VMEM),
        out_shape=jax.ShapeDtypeStruct((rows,) + corr.shape[1:], corr.dtype),
        scratch_shapes=[pltpu.SemaphoreType.DMA((16,))],
        compiler_params=pltpu.CompilerParams(vmem_limit_bytes=12 * 2**20),
        name="take",
    )(pltpu.with_memory_space_constraint(corr, pltpu.HBM))


def place_kernel(sizes, me_ref, *refs):
    pairs, row, moves, n_old, lag_groups, days, days_here = sizes
    n_blocks = len(moves)
    blocks = refs[:n_blocks]
    outs, buffers, sems = refs[n_blocks + n_old:-4], refs[-4:-1], refs[-1]
    bands = pairs // SUBLANES
    tiles = buffers[0].shape[2] // LANES
    per = LANES // (days + 2)
    my_day = me_ref[0] // lag_groups
    copies = []
    for b, (block, move) in enumerate(zip(blocks, moves)):
        sources = block.shape[0]
        for i in range(sources):
            for group in range(pl.cdiv(bands, per)):
                side = block[i, 2 * bands * tiles + group]
                scales = jnp.exp2(side - 9.0)
                for r in range(group * per, min(bands, (group + 1) * per)):
                    lane = (r - group * per) * (days + 2)
                    at = slice((i * bands + r) * SUBLANES, (i * bands + r + 1) * SUBLANES)
                    for kind in range(2):
                        scale = jnp.broadcast_to(scales[:, lane + days + kind:lane + days + kind + 1], (SUBLANES, LANES))
                        for t in range(tiles):
                            buffers[kind][b, at, t * LANES:(t + 1) * LANES] = (
                                block[i, (kind * bands + r) * tiles + t] * scale)
                    shift = (2 * LANES - lane - my_day * days_here) % LANES
                    buffers[2][b, at, :] = pltpu.roll(side, shift, 1) * (1.0 / 1024.0)
        rows = sources * pairs
        first = row
        if move is not None:
            first = pl.multiple_of(row + (my_day ^ move) * rows, SUBLANES)
        for k in range(3):
            copy = pltpu.make_async_copy(buffers[k].at[b], outs[k].at[pl.ds(first, rows), :], sems.at[k, b])
            copy.start()
            copies.append(copy)
    for copy in copies:
        copy.wait()


def place(outs, blocks, moves, me, shapes, row, pairs, lag_groups, days, days_here):
    blocks = [b.astype(jnp.float32) for b in blocks]
    rows = blocks[0].shape[0] * pairs
    n = len(blocks)
    old = list(outs or [])
    return pl.pallas_call(
        functools.partial(place_kernel, (pairs, row, moves, len(old), lag_groups, days, days_here)),
        in_specs=[pl.BlockSpec(memory_space=pltpu.SMEM)] + [pl.BlockSpec(memory_space=pltpu.VMEM)] * n
        + [pl.BlockSpec(memory_space=pl.ANY)] * len(old),
        out_specs=[pl.BlockSpec(memory_space=pl.ANY)] * 3,
        out_shape=[jax.ShapeDtypeStruct(shape, jnp.float32) for shape in shapes],
        input_output_aliases={1 + n + k: k for k in range(len(old))},
        scratch_shapes=[pltpu.VMEM((n, rows, shape[1]), jnp.float32) for shape in shapes] + [pltpu.SemaphoreType.DMA((3, n))],
        cost_estimate=pl.CostEstimate(flops=4 * n * rows * shapes[0][1], bytes_accessed=16 * n * rows * shapes[0][1], transcendentals=0),
        compiler_params=pltpu.CompilerParams(vmem_limit_bytes=20 * 2**20),
        name="place",
    )(me.reshape(1), *blocks, *old)


AXES = ("day", "lag")


def swap(x, n, by):
    return lax.ppermute(x, AXES, [(i, i ^ by) for i in range(n)])


def unswap(pieces, index):
    step = 1
    while step < len(pieces):
        odd = (index // step) % 2 == 1
        pieces = [jnp.where(odd, pieces[k ^ step], pieces[k]) for k in range(len(pieces))]
        step *= 2
    return pieces


def spread_lags(message, me, lag_groups, n):
    lag = me % lag_groups
    pieces = unswap([message[m] for m in range(lag_groups)], lag)
    got = [pieces[0]] + [swap(pieces[m], n, m) for m in range(1, lag_groups)]
    return jnp.stack(unswap(got, lag))


def spread_days(mine, lag_groups, n):
    far = swap(mine, n, 2 * lag_groups)
    near = swap(mine, n, lag_groups)
    last = swap(far, n, lag_groups)
    return (0, 2, 1, 3), (mine, far, near, last)


def per_device(corr):
    pairs, days_here, width = corr.shape
    lag_groups = lax.axis_size("lag")
    day_groups = lax.axis_size("day")
    n = lag_groups * day_groups
    me = lax.axis_index(AXES)
    lags = width * lag_groups
    days = days_here * day_groups
    tiles = width // LANES
    top = kernel_rows(min(256, lags), lags)
    mine = pairs // n
    staged = day_groups == 4 and lag_groups == 4 and mine == sum(p for p, _, _ in PLAN)
    plan = PLAN if staged else ((mine, "all", "all"),)

    def flat(piece, lead):
        piece = piece.reshape(lead + (piece.shape[-3], days_here, tiles, LANES))
        piece = jnp.swapaxes(piece, -2, -3)
        return piece.reshape(lead + (-1, LANES))

    starts = [sum(p for p, _, _ in plan[:k]) for k in range(len(plan))]
    moved, sent = [], []

    def work(k):
        message = stack_pairs(me, moved[k], top, lag_groups, days_here, plan[k][0], plan[k][0] if plan[k][0] <= 32 else (16 if plan[k][0] % 16 == 0 else 8), n,
                              1 if plan[k][2] == "staged" else day_groups)
        message = message.astype(jnp.float16)
        if plan[k][2] == "staged":
            message = spread_lags(message, me, lag_groups, n)
        sent.append(message)

    for k, (p, how, _) in enumerate(plan):
        if k == 1:
            corr, top = lax.optimization_barrier((corr, top))
        rows = corr[starts[k] * n:(starts[k] + p) * n] if k else take(corr, p * n)
        if how == "swap":
            pieces = [lax.dynamic_slice_in_dim(rows, (me ^ s) * p, p, 0) for s in range(n)]
            pieces = [pieces[0]] + [swap(pieces[s], n, s) for s in range(1, n)]
            moved.append([flat(piece, ()) for piece in pieces])
            continue
        if k >= 1:
            rows, moved[0] = lax.optimization_barrier((rows, moved[0]))
        got = lax.all_to_all(rows, AXES, 0, 0, tiled=True)
        moved.append([flat(got.reshape(n, p, days_here, width), (n,))])
    for k in range(len(sent), len(plan)):
        work(k)
    shapes = ((pairs, width), (pairs, width), (pairs, LANES))
    outs = None
    todo = []
    for k, (p, _, how) in enumerate(plan):
        if how == "all":
            turns = [((None,), (lax.all_to_all(sent[k], AXES, 0, 0, tiled=True),))]
        else:
            moves, blocks = spread_days(sent[k], lag_groups, n)
            turns = [(moves[:3], blocks[:3]), (moves[3:], blocks[3:])]
        todo.append((k, turns))
    turns_of = {k: list(turns) for k, turns in todo}
    last = len(plan) - 1
    sequence = [(k, 0) for k in range(last)] + [(k, 1) for k in range(last)] + [(last, 0)]
    for k, turn in sequence:
        moves, blocks = turns_of[k][turn]
        outs = place(outs, blocks, moves, me, shapes, starts[k] * n, plan[k][0], lag_groups, days, days_here)
    return outs[0], outs[1], outs[2][:, :days_here]


def solution(mesh):
    return jax.shard_map(
        per_device,
        mesh=mesh,
        in_specs=(P("pair", "day", "lag"),),
        out_specs=(P("pair", "lag"), P("pair", "lag"), P("pair", "day")),
        check_vma=False,
    )
```
